32 devices in a mesh: groups: 2 (over y), tensor: 4 (over z), section: 4 (over x, core).
Axes of the slice: x: 2, y: 2, z: 4, core: 2. Of those that a mesh axis runs over, the one named last changes fastest.
Arguments:
- prefill_x: bfloat16 [4096, 8192], P(('groups', 'section'), 'tensor'), parts along dimension 0, may hold values from -6 to 6
- norm_gain: float32 [8192], replicated, may hold values from 0.5 to 2
- w_q: bfloat16 [8192, 8192], P(None, 'tensor'), may hold values from -127 to 127, as said below
- q_scale: float32 [8192], P('tensor'), may hold values from 7.7339806e-05 to 0.00030935922
- key_value_weight: bfloat16 [8192, 2048], P(None, 'tensor'), may hold values from -127 to 127, as said below
- key_value_scale: float32 [2048], P('tensor'), may hold values from 7.7339806e-05 to 0.00030935922
- w_o: bfloat16 [8192, 8192], P('tensor'), may hold values from -127 to 127, as said below
- o_scale: float32 [8192], P('tensor'), may hold values from 0.0022097088 to 0.008838835
- prefix_cache: bfloat16 [4, 32, 2048, 512], P('tensor', ('groups', 'section')), parts along dimension 1, may hold values from -2048 to 2048, as said below
- prefix_len: int32 [32], P(('groups', 'section')), parts along dimension 0, may hold values from 512 to 2048, as said below
- dec_x: bfloat16 [2, 256, 8192], P(None, ('groups', 'section'), 'tensor'), parts along dimension 1, may hold values from -6 to 6
- dec_cache: bfloat16 [4, 256, 64, 512], P('tensor', ('groups', 'section')), parts along dimension 1, may hold values from -2048 to 2048, as said below
- dec_len: int32 [256], P(('groups', 'section')), parts along dimension 0, may hold values from 16 to 64, as said below
- place: int32 [32], P('groups'), parts along dimension 0, may hold values from 0 to 127, as said below
Outputs:
- prefill_out: bfloat16 [4096, 8192], P(('groups', 'section'), 'tensor'), parts along dimension 0
- decode_out: bfloat16 [2, 256, 8192], P(None, ('groups', 'section'), 'tensor'), parts along dimension 1
The draws below stay inside these ranges and needn't reach their ends.
There are 2 independent parts, one for each index of `groups`. The reference program is written for one: setup_inputs(seed, part) draws one part's arguments, and reference() takes and returns one part's arrays. A program takes and returns all parts, laid end to end along the dimension named above; an argument that names none is the same for every part. Nothing has to cross between parts.
Inputs may be any that keep to these rules, and one draw needn't show every extreme that they name: `w_q`: integers, int8 weight values. `key_value_weight`: integers, int8 weight values. `w_o`: integers, int8 weight values. `prefix_cache`: copies of one kv head on different tensor indices are equal. `dec_cache`: copies of one kv head on different tensor indices are equal. `prefix_len`: some prompt has exactly 2048 live positions. `dec_len`: some decode row has exactly 64 live positions. place[s * 4 + p] = o * 32 + r sends prompt p of section index s to decode row r of owner section index o; no two prompts share a decode row; one section index sends at most 2 prompts to one owner, and in every draw some owner receives 2 prompts from every section index.
All inputs are finite; a program needn't handle non-finite values.
Results may differ from the reference program's by a relative error of at most 0.024.
Values may be sent and summed in bfloat16 or wider, within the bound.
A program may use at most 192 MiB of HBM per device.

```python
import math
import jax
import jax.numpy as jnp
from jax import lax

MODEL_WIDTH = 8192
HQ = 64
KEY_VALUE_HEADS = 8
HEAD_SIZE = 128
PROMPT_TOKENS = 128
PROMPTS = 4
PREFIX = 2048
DROWS = 32
DCTX = 64
CAP = 2
HQD = 16
KVH_DEV = 2
N_TENSOR = 4
N_SECTION = 4


def integer_matrix(key, row_count, column_count):
    return jax.random.randint(key, (row_count, column_count), -127, 128).astype(jnp.float32).astype(jnp.bfloat16)


def draw_w_q(key, part):
    return integer_matrix(jax.random.fold_in(key, 21), MODEL_WIDTH, HQ * HEAD_SIZE)


def draw_key_value_weight(key, part):
    return integer_matrix(jax.random.fold_in(key, 22), MODEL_WIDTH, 2 * KEY_VALUE_HEADS * HEAD_SIZE)


def draw_w_o(key, part):
    return integer_matrix(jax.random.fold_in(key, 23), HQ * HEAD_SIZE, MODEL_WIDTH)


def head_cache(key, entries_count, length_total):
    starting_key = jax.random.fold_in(key, 0)
    cached_value_rows = jax.random.truncated_normal(starting_key, -5.0, 5.0, (entries_count, length_total, KEY_VALUE_HEADS, 2 * HEAD_SIZE), jnp.float32)
    return cached_value_rows.astype(jnp.bfloat16)


def tensor_copies(cached_value_rows):
    device = jnp.arange(N_TENSOR)
    head_index = device[:, None] * HQD // 8 + jnp.arange(KVH_DEV)[None, :]
    picked = cached_value_rows[:, :, head_index]
    picked = jnp.transpose(picked, (2, 0, 1, 3, 4))
    return picked.reshape(N_TENSOR, cached_value_rows.shape[0], cached_value_rows.shape[1], KVH_DEV * 2 * HEAD_SIZE)


def draw_prefix_cache(key, part):
    return tensor_copies(head_cache(jax.random.fold_in(key, 11), N_SECTION * PROMPTS, PREFIX))


def draw_dec_cache(key, part):
    return tensor_copies(head_cache(jax.random.fold_in(key, 12), N_SECTION * DROWS, DCTX))


def ragged(key, entries_count, longest):
    value_key, chosen_key = jax.random.split(key)
    values = jax.random.randint(value_key, (entries_count,), longest // 4, longest + 1)
    chosen = jax.random.randint(chosen_key, (), 0, entries_count)
    return jnp.where(jnp.arange(entries_count) == chosen, longest, values).astype(jnp.int32)


def draw_prefix_len(key, part):
    return ragged(jax.random.fold_in(key, 31), N_SECTION * PROMPTS, PREFIX)


def draw_dec_len(key, part):
    return ragged(jax.random.fold_in(key, 32), N_SECTION * DROWS, DCTX)


def draw_place(key, part):
    starting_key = jax.random.fold_in(key, 41)
    heavy_key, offset_key, order_key, row_key = jax.random.split(starting_key, 4)
    heavy_owner = jax.random.randint(heavy_key, (), 0, N_SECTION)
    offset = jax.random.randint(offset_key, (N_SECTION,), 1, N_SECTION)
    other_owner = (heavy_owner + offset) % N_SECTION
    prompt_order = jax.vmap(lambda sub: jax.random.permutation(sub, PROMPTS))(jax.random.split(order_key, N_SECTION))
    owner_section = jnp.where(prompt_order < CAP, heavy_owner, other_owner[:, None]).reshape(-1)
    owner_hits = (owner_section[:, None] == jnp.arange(N_SECTION)[None, :]).astype(jnp.int32)
    arrival_rank = jnp.sum((jnp.cumsum(owner_hits, axis=0) - owner_hits) * owner_hits, axis=1)
    row_orders = jax.vmap(lambda sub: jax.random.permutation(sub, DROWS))(jax.random.split(row_key, N_SECTION))
    decode_row = row_orders[owner_section, arrival_rank]
    return (owner_section * DROWS + decode_row).astype(jnp.int32)


def level_of(stream_key, extent, cuts, low, high):
    gain, own = 1.0, jax.random.fold_in(stream_key, 6)
    for axis_at, parts in cuts:
        steps = jnp.exp(jax.random.uniform(jax.random.fold_in(own, axis_at), (parts,), jnp.float32, low / len(cuts), high / len(cuts)))
        gain = gain * jnp.repeat(steps, extent[axis_at] // parts).reshape([-1 if axis == axis_at else 1 for axis in range(len(extent))])
    return gain


def centred(own_key, extent, width, limit, pieces=(), kind=jnp.bfloat16):
    array = width * jax.random.normal(own_key, extent, jnp.float32)
    if pieces:
        array = array * level_of(own_key, extent, pieces, -0.22, 0.18)
    return jnp.clip(array, -limit, limit).astype(kind)


def setup_inputs(seed: int = 0, part: int = 0) -> dict:
    seeds = jax.random.split(jax.random.key(seed), 15)
    part_splits = jax.random.split(jax.random.fold_in(seeds[14], part), 15)
    prefill_x = centred(part_splits[0], (N_SECTION * PROMPTS * PROMPT_TOKENS, MODEL_WIDTH), 1.0, 6.0, ((0, 4), (1, 4)))
    norm_gain = jnp.clip(jnp.exp(jax.random.uniform(seeds[1], (MODEL_WIDTH,), jnp.float32, math.log(0.5), math.log(2.0))), 0.5, 2.0)
    w_q = draw_w_q(jax.random.fold_in(seeds[14], 71), part)
    q_scale = jnp.clip(jnp.exp(math.log(0.00030935922) - 1.3862944 * jax.random.uniform(seeds[3], (HQ * HEAD_SIZE,), jnp.float32) ** level_of(seeds[3], (HQ * HEAD_SIZE,), ((0, 4),), -0.2, 0.2)), 7.733980601187795e-05, 0.00030935922)
    key_value_weight = draw_key_value_weight(jax.random.fold_in(seeds[14], 71), part)
    key_value_scale = jnp.clip(jnp.exp(math.log(0.00030935922) - 1.3862944 * jax.random.uniform(seeds[5], (2 * KEY_VALUE_HEADS * HEAD_SIZE,), jnp.float32) ** level_of(seeds[5], (2 * KEY_VALUE_HEADS * HEAD_SIZE,), ((0, 4),), -0.2, 0.2)), 7.733980601187795e-05, 0.00030935922)
    w_o = draw_w_o(jax.random.fold_in(seeds[14], 71), part)
    o_scale = jnp.clip(jnp.exp(math.log(0.008838835) - 1.3862944 * jax.random.uniform(seeds[7], (MODEL_WIDTH,), jnp.float32) ** level_of(seeds[7], (MODEL_WIDTH,), ((0, 4),), -0.2, 0.2)), 0.0022097088, 0.008838835)
    prefix_cache = draw_prefix_cache(jax.random.fold_in(jax.random.fold_in(seeds[14], part), 71), part)
    prefix_len = draw_prefix_len(jax.random.fold_in(jax.random.fold_in(seeds[14], part), 71), part)
    dec_x = centred(part_splits[10], (2, N_SECTION * DROWS, MODEL_WIDTH), 1.0, 6.0, ((1, 4), (2, 4)))
    dec_cache = draw_dec_cache(jax.random.fold_in(jax.random.fold_in(seeds[14], part), 71), part)
    dec_len = draw_dec_len(jax.random.fold_in(jax.random.fold_in(seeds[14], part), 71), part)
    place = draw_place(jax.random.fold_in(jax.random.fold_in(seeds[14], part), 71), part)
    return {"prefill_x": prefill_x, "norm_gain": norm_gain, "w_q": w_q, "q_scale": q_scale, "key_value_weight": key_value_weight, "key_value_scale": key_value_scale, "w_o": w_o, "o_scale": o_scale, "prefix_cache": prefix_cache, "prefix_len": prefix_len, "dec_x": dec_x, "dec_cache": dec_cache, "dec_len": dec_len, "place": place}


def rms_norm(activations, norm_gain):
    values = activations.astype(jnp.float32)
    mean_square = lax.optimization_barrier(jnp.mean(values * values, axis=-1, keepdims=True))
    return (values * lax.rsqrt(mean_square + 1e-05) * norm_gain).astype(jnp.bfloat16)

def project_rows(normalized_input, weight, channel_scale):
    return (jnp.dot(normalized_input, weight, preferred_element_type=jnp.float32) * channel_scale).astype(jnp.bfloat16)

def prefill_attention(queries, prefix_pages, recent_pages, live_len):
    factor = 1.0 / math.sqrt(HEAD_SIZE)
    q_float = queries.astype(jnp.float32)
    distant = jnp.einsum('pcagd,plad->pagcl', q_float, prefix_pages[:, :, :, 0].astype(jnp.float32)) * factor
    nearby = jnp.einsum('pcagd,pkad->pagck', q_float, recent_pages[:, :, :, 0].astype(jnp.float32)) * factor
    distant_live = jnp.arange(prefix_pages.shape[1])[None, :] < live_len[:, None]
    steps_new = jnp.arange(recent_pages.shape[1])
    nearby_live = steps_new[None, :] <= steps_new[:, None]
    distant = jnp.where(distant_live[:, None, None, None, :], distant, -1e+30)
    nearby = jnp.where(nearby_live[None, None, None], nearby, -1e+30)
    peak = jnp.maximum(lax.optimization_barrier(jnp.max(distant, -1, keepdims=True)), lax.optimization_barrier(jnp.max(nearby, -1, keepdims=True)))
    distant_exp = jnp.exp(distant - peak)
    nearby_exp = jnp.exp(nearby - peak)
    denominator = lax.optimization_barrier(jnp.sum(distant_exp, -1, keepdims=True)) + lax.optimization_barrier(jnp.sum(nearby_exp, -1, keepdims=True))
    distant_w = (distant_exp / denominator).astype(jnp.bfloat16).astype(jnp.float32)
    nearby_w = (nearby_exp / denominator).astype(jnp.bfloat16).astype(jnp.float32)
    attended = jnp.einsum('pagcl,plad->pcagd', distant_w, prefix_pages[:, :, :, 1].astype(jnp.float32))
    attended = attended + jnp.einsum('pagck,pkad->pcagd', nearby_w, recent_pages[:, :, :, 1].astype(jnp.float32))
    return attended.astype(jnp.bfloat16).reshape(queries.shape[0] * queries.shape[1], -1)

def decode_attention(queries, cache_pages, live_len, landed_pages, landed, fresh_pages):
    factor = 1.0 / math.sqrt(HEAD_SIZE)
    q_float = queries.astype(jnp.float32)
    distant = jnp.einsum('ragd,rlad->ragl', q_float, cache_pages[:, :, :, 0].astype(jnp.float32)) * factor
    arrival = jnp.einsum('ragd,rkad->ragk', q_float, landed_pages[:, :, :, 0].astype(jnp.float32)) * factor
    recent = jnp.einsum('ragd,rmad->ragm', q_float, fresh_pages[:, :, :, 0].astype(jnp.float32)) * factor
    distant_live = jnp.arange(cache_pages.shape[1])[None, :] < live_len[:, None]
    distant = jnp.where(distant_live[:, None, None, :], distant, -1e+30)
    arrival = jnp.where(landed[:, None, None, None], arrival, -1e+30)
    peak = jnp.maximum(lax.optimization_barrier(jnp.max(distant, -1, keepdims=True)), lax.optimization_barrier(jnp.max(arrival, -1, keepdims=True)))
    peak = jnp.maximum(peak, lax.optimization_barrier(jnp.max(recent, -1, keepdims=True)))
    distant_exp = jnp.exp(distant - peak)
    arrival_exp = jnp.exp(arrival - peak)
    recent_exp = jnp.exp(recent - peak)
    denominator = lax.optimization_barrier(jnp.sum(distant_exp, -1, keepdims=True)) + lax.optimization_barrier(jnp.sum(arrival_exp, -1, keepdims=True)) + lax.optimization_barrier(jnp.sum(recent_exp, -1, keepdims=True))
    distant_w = (distant_exp / denominator).astype(jnp.bfloat16).astype(jnp.float32)
    arrival_w = (arrival_exp / denominator).astype(jnp.bfloat16).astype(jnp.float32)
    recent_w = (recent_exp / denominator).astype(jnp.bfloat16).astype(jnp.float32)
    attended = jnp.einsum('ragl,rlad->ragd', distant_w, cache_pages[:, :, :, 1].astype(jnp.float32))
    attended = attended + jnp.einsum('ragk,rkad->ragd', arrival_w, landed_pages[:, :, :, 1].astype(jnp.float32))
    attended = attended + jnp.einsum('ragm,rmad->ragd', recent_w, fresh_pages[:, :, :, 1].astype(jnp.float32))
    return attended.astype(jnp.bfloat16).reshape(queries.shape[0], -1)

def reference(prefill_x, norm_gain, w_q, q_scale, key_value_weight, key_value_scale, w_o, o_scale, prefix_cache, prefix_len, dec_x, dec_cache, dec_len, place):
    prompts_total = N_SECTION * PROMPTS
    row_count = N_SECTION * DROWS
    page_width = KVH_DEV * 2 * HEAD_SIZE
    group_size = HQD // KVH_DEV
    normalized_input = rms_norm(prefill_x, norm_gain)
    queries = project_rows(normalized_input, w_q, q_scale).reshape(prompts_total, PROMPT_TOKENS, N_TENSOR, KVH_DEV, group_size, HEAD_SIZE)
    block_key_value = project_rows(normalized_input, key_value_weight, key_value_scale).reshape(prompts_total, PROMPT_TOKENS, 2 * KEY_VALUE_HEADS * HEAD_SIZE)
    dec_normed = rms_norm(dec_x, norm_gain)
    dec_queries = project_rows(dec_normed, w_q, q_scale).reshape(2, row_count, N_TENSOR, KVH_DEV, group_size, HEAD_SIZE)
    dec_kv = project_rows(dec_normed, key_value_weight, key_value_scale)
    arrival_hits = (place[None, :] == jnp.arange(row_count, dtype=jnp.int32)[:, None]).astype(jnp.float32)
    landed = lax.optimization_barrier(jnp.sum(arrival_hits, axis=1)) > 0.5
    out_rows = w_o.reshape(N_TENSOR, HQD * HEAD_SIZE, MODEL_WIDTH)

    def shard_terms(totals, inputs):
        device, weight_rows, prefix_pages, cache_pages = inputs
        column_start = (device * HQD // 8 * (2 * HEAD_SIZE)).astype(jnp.int32)
        own_block = lax.dynamic_slice_in_dim(block_key_value, column_start, page_width, 2)
        arrived = jnp.einsum('gp,pcw->gcw', arrival_hits, own_block.astype(jnp.float32)).astype(jnp.bfloat16)
        fresh_kv = lax.dynamic_slice_in_dim(dec_kv, column_start, page_width, 2)
        fresh_rows = jnp.transpose(fresh_kv, (1, 0, 2)).reshape(row_count, 2, KVH_DEV, 2, HEAD_SIZE)
        shard_queries = lax.dynamic_index_in_dim(queries, device, 2, keepdims=False)
        attended = prefill_attention(shard_queries, prefix_pages.reshape(prompts_total, PREFIX, KVH_DEV, 2, HEAD_SIZE), own_block.reshape(prompts_total, PROMPT_TOKENS, KVH_DEV, 2, HEAD_SIZE), prefix_len)
        shard_dec = lax.dynamic_index_in_dim(dec_queries, device, 2, keepdims=False)
        cache_rows = cache_pages.reshape(row_count, DCTX, KVH_DEV, 2, HEAD_SIZE)
        landed_rows = arrived.reshape(row_count, PROMPT_TOKENS, KVH_DEV, 2, HEAD_SIZE)
        first_step = decode_attention(shard_dec[0], cache_rows, dec_len, landed_rows, landed, fresh_rows[:, :1])
        second = decode_attention(shard_dec[1], cache_rows, dec_len, landed_rows, landed, fresh_rows)
        dec_attended = jnp.stack([first_step, second])
        prefill_term = lax.optimization_barrier(jnp.dot(attended, weight_rows, preferred_element_type=jnp.float32).astype(jnp.bfloat16)).astype(jnp.float32)
        decode_term = lax.optimization_barrier(jnp.dot(dec_attended, weight_rows, preferred_element_type=jnp.float32).astype(jnp.bfloat16)).astype(jnp.float32)
        return ((totals[0] + prefill_term, totals[1] + decode_term), None)
    initial = (jnp.zeros((prompts_total * PROMPT_TOKENS, MODEL_WIDTH), jnp.float32), jnp.zeros((2, row_count, MODEL_WIDTH), jnp.float32))
    devices = jnp.arange(N_TENSOR, dtype=jnp.int32)
    totals, unused = lax.scan(shard_terms, initial, (devices, out_rows, prefix_cache, dec_cache))
    prefill_out = (prefill_x.astype(jnp.float32) + totals[0] * o_scale).astype(jnp.bfloat16)
    decode_out = (dec_x.astype(jnp.float32) + totals[1] * o_scale).astype(jnp.bfloat16)
    return (prefill_out, decode_out)
```

```python
import math

import jax
import jax.numpy as jnp
from jax import lax
from jax.sharding import PartitionSpec as P

HEAD_SIZE = 128
PROMPT_TOKENS = 128
CHUNKS = 2


def for_sending(shard):
    return jax.tree.map(lambda a: a.astype(jnp.bfloat16) if a.dtype == jnp.float32 else a, shard)


def partner_2(block, axis, distance):
    count = lax.axis_size(axis)
    route = []
    for low in range(count):
        high = low | 1 << distance
        if high != low and high < count:
            route += [(low, high), (high, low)]
    return lax.ppermute(block, axis, route)


def rms_norm(activations, norm_gain):
    values = activations.astype(jnp.float32)
    mean_square = jnp.mean(values * values, axis=-1, keepdims=True)
    return (values * lax.rsqrt(mean_square + 1e-05) * norm_gain).astype(jnp.bfloat16)


def project_rows(normalized_input, weight, channel_scale):
    return (
        jnp.dot(normalized_input, weight, preferred_element_type=jnp.float32) * channel_scale
    ).astype(jnp.bfloat16)


def joined(portion, partner, bit_number, concat_dim, tensor_index):
    upper_half = tensor_index // 2**bit_number % 2 == 1
    lower_first = jnp.concatenate([portion, partner], axis=concat_dim)
    upper_first = jnp.concatenate([partner, portion], axis=concat_dim)
    return jnp.where(upper_half, upper_first, lower_first)


def prefill_attention(queries, prefix_pages, recent_pages, live_len):
    factor = 1.0 / math.sqrt(HEAD_SIZE)
    distant = (
        jnp.einsum(
            "pcgd,pld->pgcl",
            queries,
            prefix_pages[:, :, :HEAD_SIZE],
            preferred_element_type=jnp.float32,
        )
        * factor
    )
    nearby = (
        jnp.einsum(
            "pcgd,pkd->pgck",
            queries,
            recent_pages[:, :, :HEAD_SIZE],
            preferred_element_type=jnp.float32,
        )
        * factor
    )
    distant_live = jnp.arange(prefix_pages.shape[1])[None, :] < live_len[:, None]
    steps_new = jnp.arange(recent_pages.shape[1])
    nearby_live = steps_new[None, :] <= steps_new[:, None]
    distant = jnp.where(distant_live[:, None, None, :], distant, -1e30)
    nearby = jnp.where(nearby_live[None, None], nearby, -1e30)
    peak = jnp.maximum(jnp.max(distant, -1, keepdims=True), jnp.max(nearby, -1, keepdims=True))
    distant_exp = jnp.exp(distant - peak)
    nearby_exp = jnp.exp(nearby - peak)
    denominator = jnp.sum(distant_exp, -1, keepdims=True) + jnp.sum(nearby_exp, -1, keepdims=True)
    distant_w = (distant_exp / denominator).astype(jnp.bfloat16)
    nearby_w = (nearby_exp / denominator).astype(jnp.bfloat16)
    attended = jnp.einsum(
        "pgcl,pld->pcgd", distant_w, prefix_pages[:, :, HEAD_SIZE:], preferred_element_type=jnp.float32
    )
    attended = attended + jnp.einsum(
        "pgck,pkd->pcgd", nearby_w, recent_pages[:, :, HEAD_SIZE:], preferred_element_type=jnp.float32
    )
    return attended.astype(jnp.bfloat16).reshape(queries.shape[0] * queries.shape[1], -1)


def decode_attention(queries, cache_pages, live_len, landed_pages, landed, fresh_pages):
    factor = 1.0 / math.sqrt(HEAD_SIZE)
    distant = (
        jnp.einsum(
            "rgd,rld->rgl", queries, cache_pages[:, :, :HEAD_SIZE], preferred_element_type=jnp.float32
        )
        * factor
    )
    arrival = (
        jnp.einsum(
            "rgd,rkd->rgk", queries, landed_pages[:, :, :HEAD_SIZE], preferred_element_type=jnp.float32
        )
        * factor
    )
    recent = (
        jnp.einsum(
            "rgd,rmd->rgm", queries, fresh_pages[:, :, :HEAD_SIZE], preferred_element_type=jnp.float32
        )
        * factor
    )
    distant_live = jnp.arange(cache_pages.shape[1])[None, :] < live_len[:, None]
    distant = jnp.where(distant_live[:, None, :], distant, -1e30)
    steps = jnp.arange(queries.shape[1]) // (queries.shape[1] // fresh_pages.shape[1])
    recent_live = jnp.arange(fresh_pages.shape[1])[None, :] <= steps[:, None]
    recent = jnp.where(recent_live[None], recent, -1e30)
    arrival = jnp.where(landed[:, None, None], arrival, -1e30)
    peak = jnp.maximum(jnp.max(distant, -1, keepdims=True), jnp.max(arrival, -1, keepdims=True))
    peak = jnp.maximum(peak, jnp.max(recent, -1, keepdims=True))
    distant_exp = jnp.exp(distant - peak)
    arrival_exp = jnp.exp(arrival - peak)
    recent_exp = jnp.exp(recent - peak)
    denominator = (
        jnp.sum(distant_exp, -1, keepdims=True)
        + jnp.sum(arrival_exp, -1, keepdims=True)
        + jnp.sum(recent_exp, -1, keepdims=True)
    )
    distant_w = (distant_exp / denominator).astype(jnp.bfloat16)
    arrival_w = (arrival_exp / denominator).astype(jnp.bfloat16)
    recent_w = (recent_exp / denominator).astype(jnp.bfloat16)
    attended = jnp.einsum(
        "rgl,rld->rgd", distant_w, cache_pages[:, :, HEAD_SIZE:], preferred_element_type=jnp.float32
    )
    attended = attended + jnp.einsum(
        "rgk,rkd->rgd", arrival_w, landed_pages[:, :, HEAD_SIZE:], preferred_element_type=jnp.float32
    )
    attended = attended + jnp.einsum(
        "rgm,rmd->rgd", recent_w, fresh_pages[:, :, HEAD_SIZE:], preferred_element_type=jnp.float32
    )
    return attended.astype(jnp.bfloat16)


def scattered(partial_value, dimension):
    return lax.psum_scatter(
        partial_value, "tensor", scatter_dimension=dimension, tiled=True
    )


def exchangeable():
    count = lax.axis_size("tensor")
    return count > 2 and count & count - 1 == 0


def column_shares(partial_value):
    count = lax.axis_size("tensor")
    width = partial_value.shape[1] // count
    index = lax.axis_index("tensor")
    return {
        r: lax.dynamic_slice_in_dim(partial_value, (index ^ r) * width, width, axis=1)
        for r in range(count)
    }


def exchanged(shares, kept, bit_number):
    side = 1 << bit_number
    sums = {}
    for r in sorted(shares, reverse=True):
        if r & side:
            arriving = partner_2(shares[r], "tensor", bit_number)
            if r == side:
                kept = kept + [arriving]
            else:
                total = shares[r ^ side].astype(jnp.float32) + arriving.astype(jnp.float32)
                sums[r ^ side] = total.astype(jnp.bfloat16)
    return sums, kept


def exchange_first(partial_value):
    if not exchangeable():
        return {}, [scattered(partial_value, 1)]
    shares = column_shares(partial_value)
    kept = [shares.pop(0)]
    return exchanged(shares, kept, 0)


def exchange_rest(shares, kept):
    bit_number = 1
    while shares:
        shares, kept = exchanged(shares, kept, bit_number)
        bit_number += 1
    return kept


def residual(activations, terms, o_scale):
    total = terms[0].astype(jnp.float32)
    for term in terms[1:]:
        total = total + term.astype(jnp.float32)
    return (activations.astype(jnp.float32) + total * o_scale).astype(jnp.bfloat16)


def shards(
    prefill_x,
    norm_gain,
    w_q,
    q_scale,
    key_value_weight,
    key_value_scale,
    w_o,
    o_scale,
    prefix_cache,
    prefix_len,
    dec_x,
    dec_cache,
    dec_len,
    place,
):
    prompts_total = prefix_cache.shape[1]
    row_count = dec_cache.shape[1]
    page_width = prefix_cache.shape[3]
    kv_heads = page_width // (2 * HEAD_SIZE)
    query_heads = w_q.shape[1] // HEAD_SIZE
    group_size = query_heads // kv_heads
    section_count = lax.axis_size("section")
    section_index = lax.axis_index("section")
    tensor_index = lax.axis_index("tensor")
    head_span = max(1, 8 // query_heads)
    span_bits = head_span.bit_length() - 1
    chunk = max(1, prompts_total // CHUNKS)
    starts = range(0, prompts_total, chunk)
    rows = chunk * PROMPT_TOKENS
    dec_count = 2 * row_count
    gathered_parts = []
    for start in starts:
        part = prefill_x[start * PROMPT_TOKENS : start * PROMPT_TOKENS + rows]
        if start == 0:
            part = jnp.concatenate([dec_x.reshape(dec_count, -1), part], axis=0)
        gathered_parts.append(lax.all_gather(part, "tensor", axis=1, tiled=True))
    head_pages = 2 * HEAD_SIZE
    pieces, recent, shares = [], [], None
    partial_value = None
    for start, gathered in zip(starts, gathered_parts):
        if partial_value is not None:
            gathered, partial_value = lax.optimization_barrier((gathered, partial_value))
            shares, kept = exchange_first(partial_value)
        normed = rms_norm(gathered, norm_gain)
        kv_part = project_rows(normed, key_value_weight, key_value_scale)
        for bit_number in range(span_bits):
            partner = partner_2(for_sending(kv_part), "tensor", bit_number).astype(kv_part.dtype)
            kv_part = joined(kv_part, partner, bit_number, 1, tensor_index)
        projected = project_rows(normed, w_q, q_scale)
        if shares is not None:
            projected, shares = lax.optimization_barrier((projected, shares))
            pieces.append(exchange_rest(shares, kept))
        if start == 0:
            dec_queries = projected[:dec_count].reshape(
                2, row_count, kv_heads, group_size, HEAD_SIZE
            )
            fresh_kv = kv_part[:dec_count].reshape(2, row_count, page_width)
            projected, kv_part = projected[dec_count:], kv_part[dec_count:]
        chunk_queries = projected.reshape(-1, PROMPT_TOKENS, kv_heads, group_size, HEAD_SIZE)
        recent.append(kv_part.reshape(-1, PROMPT_TOKENS, page_width))
        attended = []
        for offset in range(chunk):
            prompt = slice(start + offset, start + offset + 1)
            for head in range(kv_heads):
                columns = slice(head * head_pages, (head + 1) * head_pages)
                attended.append(
                    prefill_attention(
                        chunk_queries[offset : offset + 1, :, head],
                        prefix_cache[0, prompt, :, columns],
                        recent[-1][offset : offset + 1, :, columns],
                        prefix_len[prompt],
                    )
                )
        attended = jnp.concatenate(
            [
                jnp.concatenate(attended[at : at + kv_heads], axis=1)
                for at in range(0, len(attended), kv_heads)
            ],
            axis=0,
        )
        partial_value = jnp.dot(attended, w_o, preferred_element_type=jnp.float32).astype(
            jnp.bfloat16
        )
    own_block = jnp.concatenate(recent, axis=0)
    owners = (place // row_count).reshape(section_count, prompts_total)
    targets = (place % row_count).reshape(section_count, prompts_total)
    owner_hits = (owners[:, :, None] == jnp.arange(section_count)[None, None, :]).astype(jnp.int32)
    slot_ranks = jnp.sum((jnp.cumsum(owner_hits, axis=1) - owner_hits) * owner_hits, axis=2)
    capacity = prompts_total // 2
    slot_ids = jnp.arange(capacity)
    sending = lax.dynamic_index_in_dim(owner_hits, section_index, 0, keepdims=False)
    my_ranks = lax.dynamic_index_in_dim(slot_ranks, section_index, 0, keepdims=False)
    selector = (
        jnp.transpose(sending)[:, None, :] * (my_ranks[None, None, :] == slot_ids[None, :, None])
    ).astype(jnp.bfloat16)
    incoming = owners == section_index
    landing = (
        incoming[:, :, None, None]
        & (slot_ranks[:, :, None, None] == slot_ids[None, None, :, None])
        & (targets[:, :, None, None] == jnp.arange(row_count)[None, None, None, :])
    )
    landing = jnp.sum(landing.astype(jnp.int32), axis=1).astype(jnp.bfloat16)
    outgoing = jnp.einsum(
        "skp,pcw->skcw", selector, own_block, preferred_element_type=jnp.float32
    ).astype(jnp.bfloat16)
    received = lax.all_to_all(outgoing, "section", split_axis=0, concat_axis=0, tiled=True)
    received, partial_value, pieces = lax.optimization_barrier((received, partial_value, pieces))
    shares, kept = exchange_first(partial_value)
    arrived = jnp.einsum(
        "skr,skcw->rcw", landing, received, preferred_element_type=jnp.float32
    ).astype(jnp.bfloat16)
    arrived, shares = lax.optimization_barrier((arrived, shares))
    pieces.append(exchange_rest(shares, kept))
    landed = jnp.sum(landing.astype(jnp.float32), axis=(0, 1)) > 0.5
    fresh_rows = jnp.transpose(fresh_kv, (1, 0, 2))
    heads_out = []
    for head in range(kv_heads):
        columns = slice(head * head_pages, (head + 1) * head_pages)
        head_queries = jnp.transpose(dec_queries[:, :, head], (1, 0, 2, 3))
        heads_out.append(
            decode_attention(
                head_queries.reshape(row_count, 2 * group_size, HEAD_SIZE),
                dec_cache[0, :, :, columns],
                dec_len,
                arrived[:, :, columns],
                landed,
                fresh_rows[:, :, columns],
            ).reshape(row_count, 2, group_size * HEAD_SIZE)
        )
    dec_attended = jnp.transpose(jnp.concatenate(heads_out, axis=2), (1, 0, 2))
    dec_attended, pieces[-1] = lax.optimization_barrier((dec_attended, pieces[-1]))
    dec_partial = jnp.dot(dec_attended, w_o, preferred_element_type=jnp.float32).astype(jnp.bfloat16)
    prefill_out = jnp.concatenate(
        [
            residual(prefill_x[at * rows : (at + 1) * rows], terms, o_scale)
            for at, terms in enumerate(pieces)
        ],
        axis=0,
    )
    decode_out = residual(dec_x, [scattered(dec_partial, 2)], o_scale)
    return (prefill_out, decode_out)


def solution(mesh):
    in_specs = (
        P(("groups", "section"), "tensor"),
        P(),
        P(None, "tensor"),
        P("tensor"),
        P(None, "tensor"),
        P("tensor"),
        P("tensor", None),
        P("tensor"),
        P("tensor", ("groups", "section"), None, None),
        P(("groups", "section")),
        P(None, ("groups", "section"), "tensor"),
        P("tensor", ("groups", "section"), None, None),
        P(("groups", "section")),
        P("groups"),
    )
    out_specs = (P(("groups", "section"), "tensor"), P(None, ("groups", "section"), "tensor"))
    return jax.shard_map(shards, mesh=mesh, in_specs=in_specs, out_specs=out_specs, check_vma=False)
```
